32 devices in a mesh: dom: 16 (over z, y, x), tgt: 2 (over core).
Axes of the slice: x: 2, y: 2, z: 4, core: 2. Of those that a mesh axis runs over, the one named last changes fastest.
Arguments:
- positions: float32 [3, 16384], P(None, ('dom', 'tgt')), may hold values from -3 to 3
- normals: float32 [3, 16384], P(None, ('dom', 'tgt')), may hold values from -6 to 6
- weights: float32 [16384], P(('dom', 'tgt')), may hold values from 0.001 to 0.01
- density: float32 [32, 16384], P(None, ('dom', 'tgt')), may hold values from -6 to 6
- partners: int32 [16, 8], P('dom'), may hold values from 0 to 15, as said below
- band_list: int32 [16, 8, 8], P('dom'), may hold values from 0 to 7
- near_list: int32 [128, 24], P(('dom', 'tgt')), may hold values from 0 to 71
- near_count: int32 [128], P(('dom', 'tgt')), may hold values from 1 to 24, as said below
- singular: int32 [128, 24], P(('dom', 'tgt')), may hold values 0 or 1
Outputs:
- near_field: float32 [32, 16384], P(None, ('dom', 'tgt'))
The draws below stay inside these ranges and needn't reach their ends.
Inputs may be any that keep to these rules, and one draw needn't show every extreme that they name: In each matching the partners pair the partitions (the partner of a partner is the partition itself, never itself), and the 8 partners of a partition are distinct. `near_count`: 24 is reached by some target tile in every draw.
All inputs are finite; a program needn't handle non-finite values. No bound on the sum of `singular` on one device may be relied on, other than what follows from the above.
Results may differ from the reference program's by a relative error of at most 0.0041.
Values sent between devices are 32-bit elements; how exact they have to be, the bound alone decides.
A program may use at most 64 MiB of HBM per device.

```python
import math
import jax
import jax.numpy as jnp
from jax import lax

TILE = 128
RHS = 16
TT = 4
BT = 8
MAXN = 24
ROUNDS = 8
PT = 8
NPTS = 16384
N_DOM = 16


def draw_partners(key, part):
    order = jax.random.permutation(jax.random.fold_in(key, 11), N_DOM).astype(jnp.int32)
    place = jnp.argsort(order).astype(jnp.int32)
    circle = N_DOM - 1
    picked = jax.random.permutation(jax.random.fold_in(key, 12), circle).astype(jnp.int32)[:ROUNDS]
    spot = place[:, None]
    rounds_sel = picked[None, :]
    mirror = (2 * rounds_sel - spot) % circle
    mate = jnp.where(mirror == spot, circle, mirror)
    mate = jnp.where(spot == circle, rounds_sel + 0 * spot, mate)
    return order[mate].astype(jnp.int32)


def draw_near_count(key, part):
    blocks = N_DOM * PT // TT
    lowest = max(1, MAXN // 4)
    levels = jax.random.randint(jax.random.fold_in(key, 21), (blocks,), lowest, MAXN + 1)
    peak_block = jax.random.randint(jax.random.fold_in(key, 22), (), 0, blocks)
    levels = levels.at[peak_block].set(MAXN)
    spread = jax.random.randint(jax.random.fold_in(key, 23), (blocks, TT), 0, 1 << 20)
    bottom = (levels[:, None] + 1) // 2
    counts_all = bottom + spread % (levels[:, None] - bottom + 1)
    counts_all = counts_all.at[:, 0].set(levels)
    return counts_all.reshape(-1).astype(jnp.int32)


def with_ends(drawn, rng, least, high):
    spot = [jax.random.randint(jax.random.fold_in(rng, axis), (), 0, length) for axis, length in enumerate(drawn.shape)]
    longest = drawn.shape.index(max(drawn.shape))
    neighbour = spot[:longest] + [(spot[longest] + 1) % drawn.shape[longest]] + spot[longest + 1:]
    return drawn.at[tuple(spot)].set(least).at[tuple(neighbour)].set(high)


def block_scale(own_key, dims, shards, low, top_value):
    loudness, own = 1.0, jax.random.fold_in(own_key, 6)
    for axis_at, parts in shards:
        heights = jnp.exp(jax.random.uniform(jax.random.fold_in(own, axis_at), (parts,), jnp.float32, low / len(shards), top_value / len(shards)))
        loudness = loudness * jnp.repeat(heights, dims[axis_at] // parts).reshape([-1 if axis == axis_at else 1 for axis in range(len(dims))])
    return loudness


def bell_draw(own_key, dims, deviation, reach, split=(), kind=jnp.bfloat16):
    level = block_scale(own_key, dims, split, -0.22, 0.18) if split else 1.0
    array = jax.random.normal(own_key, dims, jnp.float32) * deviation * level
    return jnp.minimum(jnp.maximum(array, -reach), reach).astype(kind)


def setup_inputs(seed: int = 0) -> dict:
    streams_of = jax.random.split(jax.random.key(seed), 10)
    positions = bell_draw(streams_of[0], (3, NPTS), 0.5, 3.0, ((1, 32),), jnp.float32)
    normals = bell_draw(streams_of[1], (3, NPTS), 1.0, 6.0, ((1, 32),), jnp.float32)
    weights = jnp.clip(jnp.exp(math.log(0.01) - 2.30258502 * jax.random.uniform(streams_of[2], (NPTS,), jnp.float32) ** block_scale(streams_of[2], (NPTS,), ((0, 32),), -0.2, 0.2)), 0.001, 0.01)
    density = bell_draw(streams_of[3], (2 * RHS, NPTS), 1.0, 6.0, ((1, 32),), jnp.float32)
    partners = draw_partners(jax.random.fold_in(streams_of[9], 71), 0)
    band_list = with_ends(jax.random.randint(streams_of[5], (N_DOM, ROUNDS, BT), 0, PT), jax.random.fold_in(streams_of[5], 1), 0, PT - 1).astype(jnp.int32)
    near_list = with_ends(jax.random.randint(streams_of[6], (NPTS // TILE, MAXN), 0, PT + ROUNDS * BT), jax.random.fold_in(streams_of[6], 1), 0, (PT + ROUNDS * BT) - 1).astype(jnp.int32)
    near_count = draw_near_count(jax.random.fold_in(streams_of[9], 71), 0)
    singular = with_ends((jax.random.randint(streams_of[8], (NPTS // TILE, MAXN), 0, 3) < 1).astype(jnp.int32), jax.random.fold_in(streams_of[8], 1), 0, 1)
    return {"positions": positions, "normals": normals, "weights": weights, "density": density, "partners": partners, "band_list": band_list, "near_list": near_list, "near_count": near_count, "singular": singular}


wave_number = 6.0
coupling = 1.5
narrow_core = 0.1
wide_core = 0.4

def build_kernel(target_pos, source, valid_mask, flag_row):
    offset = source[:, 0:3, :, None] - target_pos[:, :, None, :]
    core_width = jnp.where(flag_row > 0, wide_core, narrow_core)[:, None, None]
    distance = jnp.sqrt(lax.optimization_barrier(jnp.sum(offset * offset, axis=1)) + core_width * core_width)
    inverse = 1.0 / distance
    normal_part = lax.optimization_barrier(jnp.sum(offset * source[:, 3:6, :, None], axis=1)) * inverse
    radial = inverse / (4.0 * math.pi)
    cos_part = jnp.cos(wave_number * distance) * radial
    sin_part = jnp.sin(wave_number * distance) * radial
    weight_mask = source[:, 6, :, None] * valid_mask[:, None, None]
    kernel_re = weight_mask * (normal_part * (-cos_part * inverse - wave_number * sin_part) - coupling * sin_part)
    kernel_im = weight_mask * (normal_part * (wave_number * cos_part - sin_part * inverse) + coupling * cos_part)
    return jnp.concatenate([kernel_re, kernel_im], axis=1).astype(jnp.bfloat16)

def density_side(source):
    density_bf = source[:, 7:, :].astype(jnp.bfloat16)
    half_rows = density_bf.shape[1] // 2
    real_part = density_bf[:, :half_rows]
    imag_part = density_bf[:, half_rows:]
    upper = jnp.concatenate([real_part, -imag_part], axis=2)
    lower = jnp.concatenate([imag_part, real_part], axis=2)
    return jnp.concatenate([upper, lower], axis=1)

def reference(positions, normals, weights, density, partners, band_list, near_list, near_count, singular):
    payload = jnp.concatenate([positions, normals, weights[None, :], density], axis=0)
    channels = payload.shape[0]
    n_parts = partners.shape[0]
    n_rounds = partners.shape[1]
    all_tiles = payload.reshape(channels, n_parts, PT, TILE).transpose(1, 2, 0, 3)
    round_ids = jnp.arange(n_rounds, dtype=jnp.int32)

    def one_part(part_idx):
        own_tiles = all_tiles[part_idx]
        partner_ids = partners[part_idx]
        chosen = band_list[partner_ids, round_ids]
        band_tiles = all_tiles[partner_ids[:, None], chosen].reshape(-1, channels, TILE)
        source_pool = jnp.concatenate([own_tiles, band_tiles], axis=0)
        first_tile = part_idx * PT
        near_rows = lax.dynamic_slice_in_dim(near_list, first_tile, PT, 0)
        flag_rows = lax.dynamic_slice_in_dim(singular, first_tile, PT, 0)
        tile_counts = lax.dynamic_slice_in_dim(near_count, first_tile, PT, 0)
        target_pos = own_tiles[:, 0:3, :]

        def add_entry(entry_idx, totals):
            source = source_pool[near_rows[:, entry_idx]]
            valid_mask = (entry_idx < tile_counts).astype(jnp.float32)
            kernel = build_kernel(target_pos, source, valid_mask, flag_rows[:, entry_idx])
            left_side = density_side(source)
            return totals + jnp.einsum('brs,bst->brt', left_side.astype(jnp.float32), kernel.astype(jnp.float32))
        start_sum = jnp.zeros((PT, channels - 7, TILE), jnp.float32)
        return lax.fori_loop(0, MAXN, add_entry, start_sum)
    result = lax.map(one_part, jnp.arange(n_parts, dtype=jnp.int32))
    return result.transpose(2, 0, 1, 3).reshape(channels - 7, n_parts * PT * TILE)
```

```python
import functools
import math

import jax
import jax.numpy as jnp
from jax import lax
from jax.experimental import pallas as pl
from jax.experimental.pallas import tpu as pltpu
from jax.sharding import PartitionSpec as P

TILE = 128
CHUNK = 32

wave_number = 6.0
coupling = 1.5
narrow_core = 0.1
wide_core = 0.4

SIN_POLY = (4.442882919124345, -7.308245686509064, 3.606354218433074, -0.8461116503755194, 0.10982451642926026)
COS_POLY = (1.4142134962552286, -6.978850948563789, 5.73946037690675, -1.8835579059841712, 0.3106880275217573)


def poly(coefs, z):
    total = coefs[-1]
    for c in coefs[-2::-1]:
        total = total * z + c
    return total


def gather_kernel(
    columns, depth, own_ref, all_ref, z_recv, a_recv, b_recv, s_recv, up_send, down_send, a_send, b_send, s_send, own_sem
):
    mesh_id = pl.DeviceIdType.MESH
    dom, core = lax.axis_index("dom"), lax.axis_index("tgt")
    x, y, z = dom % 2, (dom // 2) % 2, dom // 4
    half = own_ref.shape[-1] // 2
    flip = ((2 * y + 1 - x), (2 * (1 - y) + x))
    place = (2 * y + x, flip[0], flip[1], 2 * (1 - y) + 1 - x)

    def part(ref, block, h):
        return ref.at[block, :, pl.ds(h * half, half)]

    def block_of(c, zz):
        return (4 * zz + place[c]) * 2 + core

    barrier = pltpu.get_barrier_semaphore()
    peers = (((4 * z + flip[0]), core), ((4 * z + flip[1]), core), (dom, 1 - core))
    for peer in peers:
        pl.semaphore_signal(barrier, inc=1, device_id=peer, device_id_type=mesh_id)

    @pl.when(z > 0)
    def _():
        pl.semaphore_signal(barrier, inc=1, device_id=(dom - 4, core), device_id_type=mesh_id)

    @pl.when(z < depth - 1)
    def _():
        pl.semaphore_signal(barrier, inc=1, device_id=(dom + 4, core), device_id_type=mesh_id)

    own_copy = pltpu.make_async_copy(own_ref.at[0], all_ref.at[dom * 2 + core], own_sem)
    own_copy.start()
    inner = jnp.logical_and(z > 0, z < depth - 1)

    @pl.when(inner)
    def _():
        pl.semaphore_wait(barrier, 5)

    @pl.when(jnp.logical_not(inner))
    def _():
        pl.semaphore_wait(barrier, 4)

    def remote(src, dst, send, recv, device):
        return pltpu.make_async_remote_copy(
            src_ref=src, dst_ref=dst, send_sem=send, recv_sem=recv, device_id=device, device_id_type=mesh_id
        )

    def source(c, zz, h, own):
        return part(own_ref, 0, h) if own else part(all_ref, block_of(c, zz), h)

    def z_copy(zz, h, step, own):
        send = (up_send if step > 0 else down_send).at[h, zz]
        return remote(
            source(0, zz, h, own), part(all_ref, block_of(0, zz), h), send, z_recv.at[h, zz], (dom + 4 * step, core)
        )

    def a_copy(zz, h, own):
        peer = peers[0] if h == 0 else peers[1]
        return remote(
            source(0, zz, h, own), part(all_ref, block_of(0, zz), h), a_send.at[h, zz], a_recv.at[h, zz], peer
        )

    def b_copy(c, zz, h, own):
        peer = peers[1] if h == 0 else peers[0]
        col = 0 if c == 0 else (1 if h == 0 else 2)
        return remote(
            source(col, zz, h, own),
            part(all_ref, block_of(col, zz), h),
            b_send.at[h, c, zz],
            b_recv.at[h, c, zz],
            peer,
        )

    def s_copy(c, zz, h, own):
        return remote(
            source(c, zz, h, own),
            part(all_ref, block_of(c, zz), h),
            s_send.at[h, c, zz],
            s_recv.at[h, c, zz],
            peers[2],
        )

    levels = [[0]] + [[-k, k] for k in range(1, depth)]

    def each(level, body):
        for step in levels[level]:
            zz = z + step
            if step == 0:
                body(zz, 0)
            elif step < 0:
                pl.when(zz >= 0)(functools.partial(body, zz, step))
            else:
                pl.when(zz < depth)(functools.partial(body, zz, step))

    def along_z(zz, step):
        own = step == 0
        for h in range(2):
            if not own:
                z_copy(zz, h, 1, False).wait_recv()
            if step <= 0:

                @pl.when(z < depth - 1)
                def _(h=h):
                    z_copy(zz, h, 1, own).start()

            if step >= 0:

                @pl.when(z > 0)
                def _(h=h):
                    z_copy(zz, h, -1, own).start()

            a_copy(zz, h, own).start()
            b_copy(0, zz, h, own).start()
            s_copy(0, zz, h, own).start()

    def from_a(zz, step):
        for h in range(2):
            a_copy(zz, h, False).wait_recv()
            b_copy(1, zz, h, False).start()
            s_copy(1 if h == 0 else 2, zz, h, False).start()

    def from_b(zz, step):
        for h in range(2):
            b_copy(0, zz, h, False).wait_recv()
            s_copy(2 if h == 0 else 1, zz, h, False).start()

    def from_ab(zz, step):
        for h in range(2):
            b_copy(1, zz, h, False).wait_recv()
            s_copy(3, zz, h, False).start()

    for turn in range(depth + 2):
        if turn < depth:
            each(turn, along_z)
        if 1 <= turn <= depth:
            each(turn - 1, from_a)
            each(turn - 1, from_b)
        if turn >= 2:
            each(turn - 2, from_ab)

    own_copy.wait()

    def finish(zz, step):
        for h in range(2):
            if step <= 0:

                @pl.when(z < depth - 1)
                def _(h=h):
                    z_copy(zz, h, 1, False).wait_send()

            if step >= 0:

                @pl.when(z > 0)
                def _(h=h):
                    z_copy(zz, h, -1, False).wait_send()

            a_copy(zz, h, False).wait_send()
            for c in range(2):
                b_copy(c, zz, h, False).wait_send()
            for c in range(4):
                s_copy(c, zz, h, False).wait()

    for level in range(depth):
        each(level, finish)


def gather_blocks(payload, n_dom, n_tgt):
    channels, points = payload.shape
    if n_tgt != 2 or n_dom % 4 or n_dom > 16 or points % (2 * TILE):
        return lax.all_gather(payload, ("dom", "tgt"), axis=0, tiled=False)
    depth = n_dom // 4
    dma = pltpu.SemaphoreType.DMA
    return pl.pallas_call(
        functools.partial(gather_kernel, n_dom, depth),
        out_shape=jax.ShapeDtypeStruct((n_dom * n_tgt, channels, points), jnp.float32),
        in_specs=[pl.BlockSpec(memory_space=pltpu.VMEM)],
        out_specs=pl.BlockSpec(memory_space=pltpu.VMEM),
        scratch_shapes=[
            dma((2, depth)),
            dma((2, depth)),
            dma((2, 2, depth)),
            dma((2, 4, depth)),
            dma((2, depth)),
            dma((2, depth)),
            dma((2, depth)),
            dma((2, 2, depth)),
            dma((2, 4, depth)),
            dma,
        ],
        compiler_params=pltpu.CompilerParams(collective_id=0, has_side_effects=True),
    )(payload[None])


def entry_kernel(
    n_tgt, rhs2, near_ref, count_ref, flag_ref, partner_ref, band_ref, own_ref, all_ref, out_ref, xb, kbuf, left
):
    local_tiles, max_near = near_ref.shape
    band_size = band_ref.shape[1] // partner_ref.shape[1]
    part_tiles = local_tiles * n_tgt
    me = lax.axis_index("dom")
    half_rows = rhs2 // 2
    kbuf[...] = jnp.zeros_like(kbuf)

    def one_tile(t, _):
        lanes = pl.ds(pl.multiple_of(t * TILE, TILE), TILE)
        for c in range(3):
            row = own_ref[pl.ds(rhs2 + c, 1), lanes]
            xb[c] = jnp.broadcast_to(row, (TILE, TILE)).T
        used = count_ref[t]
        left[...] = jnp.zeros_like(left)

        def locate(j):
            pick = near_ref[t, j]
            beyond = jnp.maximum(pick - part_tiles, 0)
            other = partner_ref[0, beyond // band_size]
            far_tile = band_ref[other, beyond]
            is_own = pick < part_tiles
            tile = jnp.where(is_own, pick, far_tile)
            dom = jnp.where(is_own, me, other)
            return dom * n_tgt + tile // local_tiles, tile % local_tiles

        def add_pair(i, total):
            total = total + lax.dot_general(
                left[...], kbuf[...], (((1,), (1,)), ((), ())), preferred_element_type=jnp.float32
            )
            for e in range(2):
                j = 2 * i + e
                jj = jnp.minimum(j, max_near - 1)
                block, tile = locate(jj)
                core = jnp.where(flag_ref[t, jj] > 0, wide_core, narrow_core) * wave_number
                core_sq = core * core
                valid = jnp.where(j < used, 1.0, 0.0)
                cols = pl.ds(pl.multiple_of(tile * TILE, TILE), TILE)
                real = all_ref[block, pl.ds(0, half_rows), cols]
                imag = all_ref[block, pl.ds(half_rows, half_rows), cols]
                base = 2 * TILE * e
                left[:half_rows, base : base + TILE] = (-real).astype(jnp.bfloat16)
                left[:half_rows, base + TILE : base + 2 * TILE] = (-imag).astype(jnp.bfloat16)
                left[half_rows:, base : base + TILE] = (-imag).astype(jnp.bfloat16)
                left[half_rows:, base + TILE : base + 2 * TILE] = real.astype(jnp.bfloat16)
                rows = [
                    jnp.broadcast_to(all_ref[block, pl.ds(rhs2 + c, 1), cols], (CHUNK, TILE)) for c in range(7)
                ]
                weight = rows[6] * valid
                for k in range(TILE // CHUNK):
                    part = pl.ds(k * CHUNK, CHUNK)
                    dx = rows[0] - xb[0, part]
                    dy = rows[1] - xb[1, part]
                    dz = rows[2] - xb[2, part]
                    d_sq = (dx * dx + core_sq) + (dy * dy + dz * dz)
                    along = dx * rows[3] + dy * rows[4] + dz * rows[5]
                    inverse = lax.rsqrt(d_sq)
                    turns = d_sq * (inverse * (0.5 / math.pi))
                    frac = turns - jnp.round(turns)
                    z = frac * frac
                    s = frac * poly(SIN_POLY, z)
                    sin = s * poly(COS_POLY, z)
                    cos = 1.0 - s * s
                    slope = along * inverse
                    radial = inverse * weight
                    a = slope * inverse * radial
                    b = (slope + coupling) * radial
                    kbuf[part, base : base + TILE] = (cos * a + sin * b).astype(jnp.bfloat16)
                    kbuf[part, base + TILE : base + 2 * TILE] = (cos * b - sin * a).astype(jnp.bfloat16)
            return total

        total = lax.fori_loop(0, (used + 1) // 2, add_pair, jnp.zeros((rhs2, TILE), jnp.float32))
        total = total + lax.dot_general(
            left[...], kbuf[...], (((1,), (1,)), ((), ())), preferred_element_type=jnp.float32
        )
        out_ref[:, lanes] = total
        return 0

    lax.fori_loop(0, local_tiles, one_tile, 0)


def shards(
    positions, normals, weights, density, partners, band_list, near_list, near_count, singular
):
    n_dom, n_tgt = lax.axis_size("dom"), lax.axis_size("tgt")
    points = positions.shape[1]
    rhs2 = density.shape[0]
    rounds, band_size = band_list.shape[1:]
    bands = rounds * band_size
    band_row = jnp.pad(band_list.reshape(1, bands).astype(jnp.float32), ((0, 0), (0, points - bands)))
    payload = jnp.concatenate(
        [
            density,
            positions * wave_number,
            normals * wave_number,
            weights[None, :] * (wave_number / (4.0 * math.pi)),
            band_row,
        ],
        axis=0,
    )
    blocks = gather_blocks(payload, n_dom, n_tgt)
    bands_all = blocks[::n_tgt, rhs2 + 7, :bands].astype(jnp.int32)
    smem = pl.BlockSpec(memory_space=pltpu.SMEM)
    vmem = pl.BlockSpec(memory_space=pltpu.VMEM)
    return pl.pallas_call(
        functools.partial(entry_kernel, n_tgt, rhs2),
        out_shape=jax.ShapeDtypeStruct((rhs2, points), jnp.float32),
        in_specs=[smem] * 5 + [vmem] * 2,
        out_specs=vmem,
        scratch_shapes=[
            pltpu.VMEM((3, TILE, TILE), jnp.float32),
            pltpu.VMEM((TILE, 4 * TILE), jnp.bfloat16),
            pltpu.VMEM((rhs2, 4 * TILE), jnp.bfloat16),
        ],
    )(near_list, near_count, singular, partners, bands_all, payload, blocks)


def solution(mesh):
    in_specs = (
        P(None, ("dom", "tgt")),
        P(None, ("dom", "tgt")),
        P(("dom", "tgt")),
        P(None, ("dom", "tgt")),
        P("dom", None),
        P("dom", None, None),
        P(("dom", "tgt"), None),
        P(("dom", "tgt")),
        P(("dom", "tgt"), None),
    )
    out_specs = P(None, ("dom", "tgt"))
    return jax.shard_map(shards, mesh=mesh, in_specs=in_specs, out_specs=out_specs, check_vma=False)
```

```python
import functools
import math

import jax
import jax.numpy as jnp
from jax import lax
from jax.experimental import pallas as pl
from jax.experimental.pallas import tpu as pltpu
from jax.sharding import PartitionSpec as P

TILE = 128
CHUNK = 32

wave_number = 6.0
coupling = 1.5
narrow_core = 0.1
wide_core = 0.4

SIN_POLY = (4.442882919124345, -7.308245686509064, 3.606354218433074, -0.8461116503755194, 0.10982451642926026)
COS_POLY = (1.4142134962552286, -6.978850948563789, 5.73946037690675, -1.8835579059841712, 0.3106880275217573)


def poly(coefs, z):
    total = coefs[-1]
    for c in coefs[-2::-1]:
        total = total * z + c
    return total


def gather_kernel(
    columns, depth, own_ref, all_ref, z_recv, a_recv, b_recv, s_recv, up_send, down_send, a_send, b_send, s_send, own_sem
):
    mesh_id = pl.DeviceIdType.MESH
    dom, core = lax.axis_index("dom"), lax.axis_index("tgt")
    x, y, z = dom % 2, (dom // 2) % 2, dom // 4
    half = own_ref.shape[-1] // 2
    flip = ((2 * y + 1 - x), (2 * (1 - y) + x))
    place = (2 * y + x, flip[0], flip[1], 2 * (1 - y) + 1 - x)

    def part(ref, block, h):
        return ref.at[block, :, pl.ds(h * half, half)]

    def block_of(c, zz):
        return (4 * zz + place[c]) * 2 + core

    barrier = pltpu.get_barrier_semaphore()
    peers = (((4 * z + flip[0]), core), ((4 * z + flip[1]), core), (dom, 1 - core))
    for peer in peers:
        pl.semaphore_signal(barrier, inc=1, device_id=peer, device_id_type=mesh_id)

    @pl.when(z > 0)
    def _():
        pl.semaphore_signal(barrier, inc=1, device_id=(dom - 4, core), device_id_type=mesh_id)

    @pl.when(z < depth - 1)
    def _():
        pl.semaphore_signal(barrier, inc=1, device_id=(dom + 4, core), device_id_type=mesh_id)

    own_copy = pltpu.make_async_copy(own_ref.at[0], all_ref.at[dom * 2 + core], own_sem)
    own_copy.start()
    inner = jnp.logical_and(z > 0, z < depth - 1)

    @pl.when(inner)
    def _():
        pl.semaphore_wait(barrier, 5)

    @pl.when(jnp.logical_not(inner))
    def _():
        pl.semaphore_wait(barrier, 4)

    def remote(src, dst, send, recv, device):
        return pltpu.make_async_remote_copy(
            src_ref=src, dst_ref=dst, send_sem=send, recv_sem=recv, device_id=device, device_id_type=mesh_id
        )

    def source(c, zz, h, own):
        return part(own_ref, 0, h) if own else part(all_ref, block_of(c, zz), h)

    def z_copy(zz, h, step, own):
        send = (up_send if step > 0 else down_send).at[h, zz]
        return remote(
            source(0, zz, h, own), part(all_ref, block_of(0, zz), h), send, z_recv.at[h, zz], (dom + 4 * step, core)
        )

    def a_copy(zz, h, own):
        peer = peers[0] if h == 0 else peers[1]
        return remote(
            source(0, zz, h, own), part(all_ref, block_of(0, zz), h), a_send.at[h, zz], a_recv.at[h, zz], peer
        )

    def b_copy(c, zz, h, own):
        peer = peers[1] if h == 0 else peers[0]
        col = 0 if c == 0 else (1 if h == 0 else 2)
        return remote(
            source(col, zz, h, own),
            part(all_ref, block_of(col, zz), h),
            b_send.at[h, c, zz],
            b_recv.at[h, c, zz],
            peer,
        )

    def s_copy(c, zz, h, own):
        return remote(
            source(c, zz, h, own),
            part(all_ref, block_of(c, zz), h),
            s_send.at[h, c, zz],
            s_recv.at[h, c, zz],
            peers[2],
        )

    levels = [[0]] + [[-k, k] for k in range(1, depth)]

    def each(level, body):
        for step in levels[level]:
            zz = z + step
            if step == 0:
                body(zz, 0)
            elif step < 0:
                pl.when(zz >= 0)(functools.partial(body, zz, step))
            else:
                pl.when(zz < depth)(functools.partial(body, zz, step))

    def along_z(zz, step):
        own = step == 0
        for h in range(2):
            if not own:
                z_copy(zz, h, 1, False).wait_recv()
            if step <= 0:

                @pl.when(z < depth - 1)
                def _(h=h):
                    z_copy(zz, h, 1, own).start()

            if step >= 0:

                @pl.when(z > 0)
                def _(h=h):
                    z_copy(zz, h, -1, own).start()

            a_copy(zz, h, own).start()
            b_copy(0, zz, h, own).start()
            s_copy(0, zz, h, own).start()

    def from_a(zz, step):
        for h in range(2):
            a_copy(zz, h, False).wait_recv()
            b_copy(1, zz, h, False).start()
            s_copy(1 if h == 0 else 2, zz, h, False).start()

    def from_b(zz, step):
        for h in range(2):
            b_copy(0, zz, h, False).wait_recv()
            s_copy(2 if h == 0 else 1, zz, h, False).start()

    def from_ab(zz, step):
        for h in range(2):
            b_copy(1, zz, h, False).wait_recv()
            s_copy(3, zz, h, False).start()

    for turn in range(depth + 2):
        if turn < depth:
            each(turn, along_z)
        if 1 <= turn <= depth:
            each(turn - 1, from_a)
            each(turn - 1, from_b)
        if turn >= 2:
            each(turn - 2, from_ab)

    own_copy.wait()

    def finish(zz, step):
        for h in range(2):
            if step <= 0:

                @pl.when(z < depth - 1)
                def _(h=h):
                    z_copy(zz, h, 1, False).wait_send()

            if step >= 0:

                @pl.when(z > 0)
                def _(h=h):
                    z_copy(zz, h, -1, False).wait_send()

            a_copy(zz, h, False).wait_send()
            for c in range(2):
                b_copy(c, zz, h, False).wait_send()
            for c in range(4):
                s_copy(c, zz, h, False).wait()

    for level in range(depth):
        each(level, finish)


def pack_kernel(rhs2, band_ref, pos_ref, normal_ref, weight_ref, density_ref, out_ref):
    points = out_ref.shape[-1]
    out_ref[0, :rhs2] = density_ref[...]
    out_ref[0, rhs2 : rhs2 + 3] = pos_ref[...] * wave_number
    out_ref[0, rhs2 + 3 : rhs2 + 6] = normal_ref[...] * wave_number
    out_ref[0, rhs2 + 6 : rhs2 + 7] = weight_ref[...] * (wave_number / (4.0 * math.pi))
    _, rounds, band_size = band_ref.shape
    lane = lax.broadcasted_iota(jnp.int32, (1, points), 1)
    bands = jnp.zeros((1, points), jnp.int32)
    for r in range(rounds):
        for b in range(band_size):
            bands = jnp.where(lane == r * band_size + b, band_ref[0, r, b], bands)
    out_ref[0, rhs2 + 7 : rhs2 + 8] = bands.astype(jnp.float32)


def gather_blocks(payload, n_dom, n_tgt):
    _, channels, points = payload.shape
    if n_tgt != 2 or n_dom % 4 or n_dom > 16 or points % (2 * TILE):
        return lax.all_gather(payload[0], ("dom", "tgt"), axis=0, tiled=False)
    depth = n_dom // 4
    dma = pltpu.SemaphoreType.DMA
    return pl.pallas_call(
        functools.partial(gather_kernel, n_dom, depth),
        out_shape=jax.ShapeDtypeStruct((n_dom * n_tgt, channels, points), jnp.float32),
        in_specs=[pl.BlockSpec(memory_space=pltpu.VMEM)],
        out_specs=pl.BlockSpec(memory_space=pltpu.VMEM),
        scratch_shapes=[
            dma((2, depth)),
            dma((2, depth)),
            dma((2, 2, depth)),
            dma((2, 4, depth)),
            dma((2, depth)),
            dma((2, depth)),
            dma((2, depth)),
            dma((2, 2, depth)),
            dma((2, 4, depth)),
            dma,
        ],
        compiler_params=pltpu.CompilerParams(collective_id=0, has_side_effects=True, vmem_limit_bytes=8 << 20),
    )(payload)


def entry_kernel(
    n_tgt, rhs2, band_size, near_ref, count_ref, flag_ref, partner_ref, own_ref, all_ref, out_ref, xb, kbuf, left, band_ref, band_sem
):
    local_tiles, max_near = near_ref.shape
    rounds = partner_ref.shape[1]
    part_tiles = local_tiles * n_tgt
    me = lax.axis_index("dom")
    half_rows = rhs2 // 2
    copies = [
        pltpu.make_async_copy(
            all_ref.at[partner_ref[0, r] * n_tgt, rhs2 + 7, pl.ds(0, band_ref.shape[1])], band_ref.at[r], band_sem.at[r]
        )
        for r in range(rounds)
    ]
    for copy in copies:
        copy.start()
    kbuf[...] = jnp.zeros_like(kbuf)
    for copy in copies:
        copy.wait()

    def one_tile(t, _):
        lanes = pl.ds(pl.multiple_of(t * TILE, TILE), TILE)
        for c in range(3):
            row = own_ref[0, pl.ds(rhs2 + c, 1), lanes]
            xb[c] = jnp.broadcast_to(row, (TILE, TILE)).T
        used = count_ref[t]
        left[...] = jnp.zeros_like(left)

        def locate(j):
            pick = near_ref[t, j]
            beyond = jnp.maximum(pick - part_tiles, 0)
            other = partner_ref[0, beyond // band_size]
            far_tile = band_ref[beyond // band_size, beyond].astype(jnp.int32)
            is_own = pick < part_tiles
            tile = jnp.where(is_own, pick, far_tile)
            dom = jnp.where(is_own, me, other)
            return dom * n_tgt + tile // local_tiles, tile % local_tiles

        def add_pair(i, total):
            total = total + lax.dot_general(
                left[...], kbuf[...], (((1,), (1,)), ((), ())), preferred_element_type=jnp.float32
            )
            for e in range(2):
                j = 2 * i + e
                jj = jnp.minimum(j, max_near - 1)
                block, tile = locate(jj)
                core = jnp.where(flag_ref[t, jj] > 0, wide_core, narrow_core) * wave_number
                core_sq = core * core
                valid = jnp.where(j < used, 1.0, 0.0)
                cols = pl.ds(pl.multiple_of(tile * TILE, TILE), TILE)
                real = all_ref[block, pl.ds(0, half_rows), cols]
                imag = all_ref[block, pl.ds(half_rows, half_rows), cols]
                base = 2 * TILE * e
                left[:half_rows, base : base + TILE] = (-real).astype(jnp.bfloat16)
                left[:half_rows, base + TILE : base + 2 * TILE] = (-imag).astype(jnp.bfloat16)
                left[half_rows:, base : base + TILE] = (-imag).astype(jnp.bfloat16)
                left[half_rows:, base + TILE : base + 2 * TILE] = real.astype(jnp.bfloat16)
                rows = [
                    jnp.broadcast_to(all_ref[block, pl.ds(rhs2 + c, 1), cols], (CHUNK, TILE)) for c in range(7)
                ]
                weight = rows[6] * valid
                for k in range(TILE // CHUNK):
                    part = pl.ds(k * CHUNK, CHUNK)
                    dx = rows[0] - xb[0, part]
                    dy = rows[1] - xb[1, part]
                    dz = rows[2] - xb[2, part]
                    d_sq = (dx * dx + core_sq) + (dy * dy + dz * dz)
                    along = dx * rows[3] + dy * rows[4] + dz * rows[5]
                    inverse = lax.rsqrt(d_sq)
                    turns = d_sq * (inverse * (0.5 / math.pi))
                    frac = turns - jnp.round(turns)
                    z = frac * frac
                    s = frac * poly(SIN_POLY, z)
                    sin = s * poly(COS_POLY, z)
                    cos = 1.0 - s * s
                    slope = along * inverse
                    radial = inverse * weight
                    a = slope * inverse * radial
                    b = (slope + coupling) * radial
                    kbuf[part, base : base + TILE] = (cos * a + sin * b).astype(jnp.bfloat16)
                    kbuf[part, base + TILE : base + 2 * TILE] = (cos * b - sin * a).astype(jnp.bfloat16)
            return total

        total = lax.fori_loop(0, (used + 1) // 2, add_pair, jnp.zeros((rhs2, TILE), jnp.float32))
        total = total + lax.dot_general(
            left[...], kbuf[...], (((1,), (1,)), ((), ())), preferred_element_type=jnp.float32
        )
        out_ref[:, lanes] = total
        return 0

    lax.fori_loop(0, local_tiles, one_tile, 0)


def shards(
    positions, normals, weights, density, partners, band_list, near_list, near_count, singular
):
    n_dom, n_tgt = lax.axis_size("dom"), lax.axis_size("tgt")
    points = positions.shape[1]
    rhs2 = density.shape[0]
    rounds, band_size = band_list.shape[1:]
    bands = rounds * band_size
    smem = pl.BlockSpec(memory_space=pltpu.SMEM)
    vmem = pl.BlockSpec(memory_space=pltpu.VMEM)
    payload = pl.pallas_call(
        functools.partial(pack_kernel, rhs2),
        out_shape=jax.ShapeDtypeStruct((1, rhs2 + 8, points), jnp.float32),
        in_specs=[smem] + [vmem] * 4,
        out_specs=vmem,
        compiler_params=pltpu.CompilerParams(vmem_limit_bytes=4 << 20),
    )(band_list, positions, normals, weights[None, :], density)
    blocks = gather_blocks(payload, n_dom, n_tgt)
    band_lanes = -(-bands // TILE) * TILE
    return pl.pallas_call(
        functools.partial(entry_kernel, n_tgt, rhs2, band_size),
        out_shape=jax.ShapeDtypeStruct((rhs2, points), jnp.float32),
        in_specs=[smem] * 4 + [vmem] * 2,
        out_specs=vmem,
        scratch_shapes=[
            pltpu.VMEM((3, TILE, TILE), jnp.float32),
            pltpu.VMEM((TILE, 4 * TILE), jnp.bfloat16),
            pltpu.VMEM((rhs2, 4 * TILE), jnp.bfloat16),
            pltpu.SMEM((rounds, band_lanes), jnp.float32),
            pltpu.SemaphoreType.DMA((rounds,)),
        ],
        compiler_params=pltpu.CompilerParams(vmem_limit_bytes=4 * blocks.size + (6 << 20)),
    )(near_list, near_count, singular, partners, payload, blocks)


def solution(mesh):
    in_specs = (
        P(None, ("dom", "tgt")),
        P(None, ("dom", "tgt")),
        P(("dom", "tgt")),
        P(None, ("dom", "tgt")),
        P("dom", None),
        P("dom", None, None),
        P(("dom", "tgt"), None),
        P(("dom", "tgt")),
        P(("dom", "tgt"), None),
    )
    out_specs = P(None, ("dom", "tgt"))
    return jax.shard_map(shards, mesh=mesh, in_specs=in_specs, out_specs=out_specs, check_vma=False)
```

```python
import functools
import math

import jax
import jax.numpy as jnp
from jax import lax
from jax.experimental import pallas as pl
from jax.experimental.pallas import tpu as pltpu
from jax.sharding import PartitionSpec as P

TILE = 128
CHUNK = 32

wave_number = 6.0
coupling = 1.5
narrow_core = 0.1
wide_core = 0.4

SIN_POLY = (4.442882919124345, -7.308245686509064, 3.606354218433074, -0.8461116503755194, 0.10982451642926026)
COS_POLY = (1.4142134962552286, -6.978850948563789, 5.73946037690675, -1.8835579059841712, 0.3106880275217573)


def poly(coefs, z):
    total = coefs[-1]
    for c in coefs[-2::-1]:
        total = total * z + c
    return total


def gather_kernel(
    columns, depth, own_ref, all_ref, z_recv, a_recv, b_recv, s_recv, up_send, down_send, a_send, b_send, s_send, own_sem,
    z2_recv, a2_recv, b2_recv, s2_recv, up2_send, down2_send, a2_send, b2_send, s2_send
):
    mesh_id = pl.DeviceIdType.MESH
    dom, core = lax.axis_index("dom"), lax.axis_index("tgt")
    x, y, z = dom % 2, (dom // 2) % 2, dom // 4
    half = own_ref.shape[-1] // 2
    top = own_ref.shape[1] - 8
    flip = ((2 * y + 1 - x), (2 * (1 - y) + x))
    place = (2 * y + x, flip[0], flip[1], 2 * (1 - y) + 1 - x)

    def part(ref, block, h):
        if h == 2:
            return ref.at[block, pl.ds(top, 8), :]
        return ref.at[block, pl.ds(0, top), pl.ds(h * half, half)]

    def block_of(c, zz):
        return (4 * zz + place[c]) * 2 + core

    barrier = pltpu.get_barrier_semaphore()
    peers = (((4 * z + flip[0]), core), ((4 * z + flip[1]), core), (dom, 1 - core))
    for peer in peers:
        pl.semaphore_signal(barrier, inc=1, device_id=peer, device_id_type=mesh_id)

    @pl.when(z > 0)
    def _():
        pl.semaphore_signal(barrier, inc=1, device_id=(dom - 4, core), device_id_type=mesh_id)

    @pl.when(z < depth - 1)
    def _():
        pl.semaphore_signal(barrier, inc=1, device_id=(dom + 4, core), device_id_type=mesh_id)

    own_copy = pltpu.make_async_copy(own_ref.at[0], all_ref.at[dom * 2 + core], own_sem)
    own_copy.start()
    inner = jnp.logical_and(z > 0, z < depth - 1)

    @pl.when(inner)
    def _():
        pl.semaphore_wait(barrier, 5)

    @pl.when(jnp.logical_not(inner))
    def _():
        pl.semaphore_wait(barrier, 4)

    def remote(src, dst, send, recv, device):
        return pltpu.make_async_remote_copy(
            src_ref=src, dst_ref=dst, send_sem=send, recv_sem=recv, device_id=device, device_id_type=mesh_id
        )

    def source(c, zz, h, own):
        return part(own_ref, 0, h) if own else part(all_ref, block_of(c, zz), h)

    def z_copy(zz, h, step, own):
        send = (up_send if step > 0 else down_send).at[h, zz]
        return remote(
            source(0, zz, h, own), part(all_ref, block_of(0, zz), h), send, z_recv.at[h, zz], (dom + 4 * step, core)
        )

    def a_copy(zz, h, own):
        peer = peers[0] if h == 0 else peers[1]
        return remote(
            source(0, zz, h, own), part(all_ref, block_of(0, zz), h), a_send.at[h, zz], a_recv.at[h, zz], peer
        )

    def b_copy(c, zz, h, own):
        peer = peers[1] if h == 0 else peers[0]
        col = 0 if c == 0 else (1 if h == 0 else 2)
        return remote(
            source(col, zz, h, own),
            part(all_ref, block_of(col, zz), h),
            b_send.at[h, c, zz],
            b_recv.at[h, c, zz],
            peer,
        )

    def s_copy(c, zz, h, own):
        return remote(
            source(c, zz, h, own),
            part(all_ref, block_of(c, zz), h),
            s_send.at[h, c, zz],
            s_recv.at[h, c, zz],
            peers[2],
        )

    def z2_copy(c, zz, step, own):
        send = (up2_send if step > 0 else down2_send).at[c, zz]
        return remote(
            source(c, zz, 2, own), part(all_ref, block_of(c, zz), 2), send, z2_recv.at[c, zz], (dom + 4 * step, core)
        )

    def a2_copy(own):
        return remote(source(0, z, 2, own), part(all_ref, block_of(0, z), 2), a2_send, a2_recv, peers[0])

    def b2_copy(c, own):
        return remote(source(c, z, 2, own), part(all_ref, block_of(c, z), 2), b2_send.at[c], b2_recv.at[c], peers[1])

    def s2_copy(c, zz, own):
        return remote(
            source(c, zz, 2, own), part(all_ref, block_of(c, zz), 2), s2_send.at[c, zz], s2_recv.at[c, zz], peers[2]
        )

    def spread2(c, own):
        @pl.when(z < depth - 1)
        def _():
            z2_copy(c, z, 1, own).start()

        @pl.when(z > 0)
        def _():
            z2_copy(c, z, -1, own).start()

        s2_copy(c, z, own).start()

    def along_z2(zz, step):
        for c in range(4):
            z2_copy(c, zz, 1, False).wait_recv()
            if step < 0:

                @pl.when(z < depth - 1)
                def _(c=c):
                    z2_copy(c, zz, 1, False).start()

            else:

                @pl.when(z > 0)
                def _(c=c):
                    z2_copy(c, zz, -1, False).start()

            s2_copy(c, zz, False).start()

    levels = [[0]] + [[-k, k] for k in range(1, depth)]

    def each(level, body):
        for step in levels[level]:
            zz = z + step
            if step == 0:
                body(zz, 0)
            elif step < 0:
                pl.when(zz >= 0)(functools.partial(body, zz, step))
            else:
                pl.when(zz < depth)(functools.partial(body, zz, step))

    def along_z(zz, step):
        own = step == 0
        for h in range(2):
            if not own:
                z_copy(zz, h, 1, False).wait_recv()
            if step <= 0:

                @pl.when(z < depth - 1)
                def _(h=h):
                    z_copy(zz, h, 1, own).start()

            if step >= 0:

                @pl.when(z > 0)
                def _(h=h):
                    z_copy(zz, h, -1, own).start()

            a_copy(zz, h, own).start()
            b_copy(0, zz, h, own).start()
            s_copy(0, zz, h, own).start()

    def from_a(zz, step):
        for h in range(2):
            a_copy(zz, h, False).wait_recv()
            b_copy(1, zz, h, False).start()
            s_copy(1 if h == 0 else 2, zz, h, False).start()

    def from_b(zz, step):
        for h in range(2):
            b_copy(0, zz, h, False).wait_recv()
            s_copy(2 if h == 0 else 1, zz, h, False).start()

    def from_ab(zz, step):
        for h in range(2):
            b_copy(1, zz, h, False).wait_recv()
            s_copy(3, zz, h, False).start()

    for turn in range(depth + 2):
        if turn == 0:
            a2_copy(True).start()
            b2_copy(0, True).start()
            spread2(0, True)
        if turn == 1:
            a2_copy(False).wait_recv()
            b2_copy(1, False).start()
            spread2(1, False)
            b2_copy(0, False).wait_recv()
            spread2(2, False)
        if turn == 2:
            b2_copy(1, False).wait_recv()
            spread2(3, False)
        if turn < depth:
            each(turn, along_z)
        if 1 <= turn <= depth:
            each(turn - 1, from_a)
            each(turn - 1, from_b)
        if turn >= 3:
            each(turn - 2, along_z2)
        if turn >= 2:
            each(turn - 2, from_ab)

    own_copy.wait()

    def finish(zz, step):
        for h in range(2):
            if step <= 0:

                @pl.when(z < depth - 1)
                def _(h=h):
                    z_copy(zz, h, 1, False).wait_send()

            if step >= 0:

                @pl.when(z > 0)
                def _(h=h):
                    z_copy(zz, h, -1, False).wait_send()

            a_copy(zz, h, False).wait_send()
            for c in range(2):
                b_copy(c, zz, h, False).wait_send()
            for c in range(4):
                s_copy(c, zz, h, False).wait()
        for c in range(4):
            if step <= 0:

                @pl.when(z < depth - 1)
                def _(c=c):
                    z2_copy(c, zz, 1, False).wait_send()

            if step >= 0:

                @pl.when(z > 0)
                def _(c=c):
                    z2_copy(c, zz, -1, False).wait_send()

            s2_copy(c, zz, False).wait()

    a2_copy(False).wait_send()
    for c in range(2):
        b2_copy(c, False).wait_send()

    for level in range(depth):
        each(level, finish)


def pack_kernel(rhs2, band_hbm, pos_hbm, normal_hbm, weight_hbm, density_hbm, out_ref, band_ref, pos_ref, normal_ref, weight_ref, sems):
    pairs = (
        (band_hbm, band_ref),
        (pos_hbm, pos_ref),
        (normal_hbm, normal_ref),
        (weight_hbm, weight_ref),
        (density_hbm, out_ref.at[0, pl.ds(0, rhs2)]),
    )
    copies = [pltpu.make_async_copy(src, dst, sems.at[i]) for i, (src, dst) in enumerate(pairs)]
    for copy in copies:
        copy.start()
    for copy in copies:
        copy.wait()
    points = out_ref.shape[-1]
    out_ref[0, rhs2 : rhs2 + 3] = pos_ref[...] * wave_number
    out_ref[0, rhs2 + 3 : rhs2 + 6] = normal_ref[...] * wave_number
    out_ref[0, rhs2 + 6 : rhs2 + 7] = weight_ref[...] * (wave_number / (4.0 * math.pi))
    _, rounds, band_size = band_ref.shape
    lane = lax.broadcasted_iota(jnp.int32, (1, points), 1)
    bands = jnp.zeros((1, points), jnp.int32)
    for r in range(rounds):
        for b in range(band_size):
            bands = jnp.where(lane == r * band_size + b, band_ref[0, r, b], bands)
    out_ref[0, rhs2 + 7 : rhs2 + 8] = bands.astype(jnp.float32)


def gather_blocks(payload, n_dom, n_tgt):
    _, channels, points = payload.shape
    if n_tgt != 2 or n_dom % 4 or n_dom > 16 or points % (2 * TILE) or channels % 8:
        return lax.all_gather(payload[0], ("dom", "tgt"), axis=0, tiled=False)
    depth = n_dom // 4
    dma = pltpu.SemaphoreType.DMA
    return pl.pallas_call(
        functools.partial(gather_kernel, n_dom, depth),
        out_shape=jax.ShapeDtypeStruct((n_dom * n_tgt, channels, points), jnp.float32),
        in_specs=[pl.BlockSpec(memory_space=pltpu.VMEM)],
        out_specs=pl.BlockSpec(memory_space=pltpu.VMEM),
        scratch_shapes=[
            dma((2, depth)),
            dma((2, depth)),
            dma((2, 2, depth)),
            dma((2, 4, depth)),
            dma((2, depth)),
            dma((2, depth)),
            dma((2, depth)),
            dma((2, 2, depth)),
            dma((2, 4, depth)),
            dma,
            dma((4, depth)),
            dma,
            dma((2,)),
            dma((4, depth)),
            dma((4, depth)),
            dma((4, depth)),
            dma,
            dma((2,)),
            dma((4, depth)),
        ],
        compiler_params=pltpu.CompilerParams(collective_id=0, has_side_effects=True, vmem_limit_bytes=8 << 20),
    )(payload)


def entry_kernel(
    n_tgt, rhs2, band_size, near_ref, count_ref, flag_ref, partner_ref, own_ref, all_ref, out_ref, xb, kbuf, left, band_ref, band_sem
):
    local_tiles, max_near = near_ref.shape
    rounds = partner_ref.shape[1]
    part_tiles = local_tiles * n_tgt
    me = lax.axis_index("dom")
    half_rows = rhs2 // 2
    copies = [
        pltpu.make_async_copy(
            all_ref.at[partner_ref[0, r] * n_tgt, rhs2 + 7, pl.ds(0, band_ref.shape[1])], band_ref.at[r], band_sem.at[r]
        )
        for r in range(rounds)
    ]
    for copy in copies:
        copy.start()
    kbuf[...] = jnp.zeros_like(kbuf)
    for copy in copies:
        copy.wait()

    def one_tile(t, _):
        lanes = pl.ds(pl.multiple_of(t * TILE, TILE), TILE)
        for c in range(3):
            row = own_ref[0, pl.ds(rhs2 + c, 1), lanes]
            xb[c] = jnp.broadcast_to(row, (TILE, TILE)).T
        used = count_ref[t]
        left[...] = jnp.zeros_like(left)

        def locate(j):
            pick = near_ref[t, j]
            beyond = jnp.maximum(pick - part_tiles, 0)
            other = partner_ref[0, beyond // band_size]
            far_tile = band_ref[beyond // band_size, beyond].astype(jnp.int32)
            is_own = pick < part_tiles
            tile = jnp.where(is_own, pick, far_tile)
            dom = jnp.where(is_own, me, other)
            return dom * n_tgt + tile // local_tiles, tile % local_tiles

        def add_pair(i, total):
            total = total + lax.dot_general(
                left[...], kbuf[...], (((1,), (1,)), ((), ())), preferred_element_type=jnp.float32
            )
            for e in range(2):
                j = 2 * i + e
                jj = jnp.minimum(j, max_near - 1)
                block, tile = locate(jj)
                core = jnp.where(flag_ref[t, jj] > 0, wide_core, narrow_core) * wave_number
                core_sq = core * core
                valid = jnp.where(j < used, 1.0, 0.0)
                cols = pl.ds(pl.multiple_of(tile * TILE, TILE), TILE)
                real = all_ref[block, pl.ds(0, half_rows), cols]
                imag = all_ref[block, pl.ds(half_rows, half_rows), cols]
                base = 2 * TILE * e
                left[:half_rows, base : base + TILE] = (-real).astype(jnp.bfloat16)
                left[:half_rows, base + TILE : base + 2 * TILE] = (-imag).astype(jnp.bfloat16)
                left[half_rows:, base : base + TILE] = (-imag).astype(jnp.bfloat16)
                left[half_rows:, base + TILE : base + 2 * TILE] = real.astype(jnp.bfloat16)
                rows = [
                    jnp.broadcast_to(all_ref[block, pl.ds(rhs2 + c, 1), cols], (CHUNK, TILE)) for c in range(7)
                ]
                weight = rows[6] * valid
                for k in range(TILE // CHUNK):
                    part = pl.ds(k * CHUNK, CHUNK)
                    dx = rows[0] - xb[0, part]
                    dy = rows[1] - xb[1, part]
                    dz = rows[2] - xb[2, part]
                    d_sq = (dx * dx + core_sq) + (dy * dy + dz * dz)
                    along = dx * rows[3] + dy * rows[4] + dz * rows[5]
                    inverse = lax.rsqrt(d_sq)
                    turns = d_sq * (inverse * (0.5 / math.pi))
                    frac = turns - jnp.round(turns)
                    z = frac * frac
                    s = frac * poly(SIN_POLY, z)
                    sin = s * poly(COS_POLY, z)
                    cos = 1.0 - s * s
                    slope = along * inverse
                    radial = inverse * weight
                    a = slope * inverse * radial
                    b = (slope + coupling) * radial
                    kbuf[part, base : base + TILE] = (cos * a + sin * b).astype(jnp.bfloat16)
                    kbuf[part, base + TILE : base + 2 * TILE] = (cos * b - sin * a).astype(jnp.bfloat16)
            return total

        total = lax.fori_loop(0, (used + 1) // 2, add_pair, jnp.zeros((rhs2, TILE), jnp.float32))
        total = total + lax.dot_general(
            left[...], kbuf[...], (((1,), (1,)), ((), ())), preferred_element_type=jnp.float32
        )
        out_ref[:, lanes] = total
        return 0

    lax.fori_loop(0, local_tiles, one_tile, 0)


def shards(
    positions, normals, weights, density, partners, band_list, near_list, near_count, singular
):
    n_dom, n_tgt = lax.axis_size("dom"), lax.axis_size("tgt")
    points = positions.shape[1]
    rhs2 = density.shape[0]
    rounds, band_size = band_list.shape[1:]
    bands = rounds * band_size
    smem = pl.BlockSpec(memory_space=pltpu.SMEM)
    vmem = pl.BlockSpec(memory_space=pltpu.VMEM)
    payload = pl.pallas_call(
        functools.partial(pack_kernel, rhs2),
        out_shape=jax.ShapeDtypeStruct((1, rhs2 + 8, points), jnp.float32),
        in_specs=[pl.BlockSpec(memory_space=pltpu.HBM)] * 5,
        out_specs=vmem,
        scratch_shapes=[
            pltpu.SMEM(band_list.shape, jnp.int32),
            pltpu.VMEM(positions.shape, jnp.float32),
            pltpu.VMEM(normals.shape, jnp.float32),
            pltpu.VMEM((1, points), jnp.float32),
            pltpu.SemaphoreType.DMA((5,)),
        ],
        compiler_params=pltpu.CompilerParams(vmem_limit_bytes=4 << 20),
    )(*[pltpu.with_memory_space_constraint(a, pltpu.HBM) for a in (band_list, positions, normals, weights[None, :], density)])
    blocks = gather_blocks(payload, n_dom, n_tgt)
    band_lanes = -(-bands // TILE) * TILE
    return pl.pallas_call(
        functools.partial(entry_kernel, n_tgt, rhs2, band_size),
        out_shape=jax.ShapeDtypeStruct((rhs2, points), jnp.float32),
        in_specs=[smem] * 4 + [vmem] * 2,
        out_specs=vmem,
        scratch_shapes=[
            pltpu.VMEM((3, TILE, TILE), jnp.float32),
            pltpu.VMEM((TILE, 4 * TILE), jnp.bfloat16),
            pltpu.VMEM((rhs2, 4 * TILE), jnp.bfloat16),
            pltpu.SMEM((rounds, band_lanes), jnp.float32),
            pltpu.SemaphoreType.DMA((rounds,)),
        ],
        compiler_params=pltpu.CompilerParams(vmem_limit_bytes=4 * blocks.size + (6 << 20)),
    )(near_list, near_count, singular, partners, payload, blocks)


def solution(mesh):
    in_specs = (
        P(None, ("dom", "tgt")),
        P(None, ("dom", "tgt")),
        P(("dom", "tgt")),
        P(None, ("dom", "tgt")),
        P("dom", None),
        P("dom", None, None),
        P(("dom", "tgt"), None),
        P(("dom", "tgt")),
        P(("dom", "tgt"), None),
    )
    out_specs = P(None, ("dom", "tgt"))
    return jax.shard_map(shards, mesh=mesh, in_specs=in_specs, out_specs=out_specs, check_vma=False)
```

```python
import functools
import math

import jax
import jax.numpy as jnp
from jax import lax
from jax.experimental import pallas as pl
from jax.experimental.pallas import tpu as pltpu
from jax.sharding import PartitionSpec as P

TILE = 128
CHUNK = 32

wave_number = 6.0
coupling = 1.5
narrow_core = 0.1
wide_core = 0.4

SIN_POLY = (4.442882919124345, -7.308245686509064, 3.606354218433074, -0.8461116503755194, 0.10982451642926026)
COS_POLY = (1.4142134962552286, -6.978850948563789, 5.73946037690675, -1.8835579059841712, 0.3106880275217573)


def poly(coefs, z):
    total = coefs[-1]
    for c in coefs[-2::-1]:
        total = total * z + c
    return total


def gather_kernel(
    columns, depth, own_ref, all_ref, z_recv, a_recv, b_recv, s_recv, up_send, down_send, a_send, b_send, s_send, own_sem
):
    mesh_id = pl.DeviceIdType.MESH
    dom, core = lax.axis_index("dom"), lax.axis_index("tgt")
    x, y, z = dom % 2, (dom // 2) % 2, dom // 4
    half = own_ref.shape[1] // 2
    flip = ((2 * y + 1 - x), (2 * (1 - y) + x))
    place = (2 * y + x, flip[0], flip[1], 2 * (1 - y) + 1 - x)

    def part(ref, block, h):
        return ref.at[block, pl.ds(h * half, half)]

    def block_of(c, zz):
        return (4 * zz + place[c]) * 2 + core

    barrier = pltpu.get_barrier_semaphore()
    peers = (((4 * z + flip[0]), core), ((4 * z + flip[1]), core), (dom, 1 - core))
    for peer in peers:
        pl.semaphore_signal(barrier, inc=1, device_id=peer, device_id_type=mesh_id)

    @pl.when(z > 0)
    def _():
        pl.semaphore_signal(barrier, inc=1, device_id=(dom - 4, core), device_id_type=mesh_id)

    @pl.when(z < depth - 1)
    def _():
        pl.semaphore_signal(barrier, inc=1, device_id=(dom + 4, core), device_id_type=mesh_id)

    own_copy = pltpu.make_async_copy(own_ref.at[0], all_ref.at[dom * 2 + core], own_sem)
    own_copy.start()
    inner = jnp.logical_and(z > 0, z < depth - 1)

    @pl.when(inner)
    def _():
        pl.semaphore_wait(barrier, 5)

    @pl.when(jnp.logical_not(inner))
    def _():
        pl.semaphore_wait(barrier, 4)

    def remote(src, dst, send, recv, device):
        return pltpu.make_async_remote_copy(
            src_ref=src, dst_ref=dst, send_sem=send, recv_sem=recv, device_id=device, device_id_type=mesh_id
        )

    def source(c, zz, h, own):
        return part(own_ref, 0, h) if own else part(all_ref, block_of(c, zz), h)

    def z_copy(zz, h, step, own):
        send = (up_send if step > 0 else down_send).at[h, zz]
        return remote(
            source(0, zz, h, own), part(all_ref, block_of(0, zz), h), send, z_recv.at[h, zz], (dom + 4 * step, core)
        )

    def a_copy(zz, h, own):
        peer = peers[0] if h == 0 else peers[1]
        return remote(
            source(0, zz, h, own), part(all_ref, block_of(0, zz), h), a_send.at[h, zz], a_recv.at[h, zz], peer
        )

    def b_copy(c, zz, h, own):
        peer = peers[1] if h == 0 else peers[0]
        col = 0 if c == 0 else (1 if h == 0 else 2)
        return remote(
            source(col, zz, h, own),
            part(all_ref, block_of(col, zz), h),
            b_send.at[h, c, zz],
            b_recv.at[h, c, zz],
            peer,
        )

    def s_copy(c, zz, h, own):
        return remote(
            source(c, zz, h, own),
            part(all_ref, block_of(c, zz), h),
            s_send.at[h, c, zz],
            s_recv.at[h, c, zz],
            peers[2],
        )

    levels = [[0]] + [[-k, k] for k in range(1, depth)]

    def each(level, body):
        for step in levels[level]:
            zz = z + step
            if step == 0:
                body(zz, 0)
            elif step < 0:
                pl.when(zz >= 0)(functools.partial(body, zz, step))
            else:
                pl.when(zz < depth)(functools.partial(body, zz, step))

    def along_z(zz, step):
        own = step == 0
        for h in range(2):
            if not own:
                z_copy(zz, h, 1, False).wait_recv()
            if step <= 0:

                @pl.when(z < depth - 1)
                def _(h=h):
                    z_copy(zz, h, 1, own).start()

            if step >= 0:

                @pl.when(z > 0)
                def _(h=h):
                    z_copy(zz, h, -1, own).start()

            a_copy(zz, h, own).start()
            b_copy(0, zz, h, own).start()
            s_copy(0, zz, h, own).start()

    def from_a(zz, step):
        for h in range(2):
            a_copy(zz, h, False).wait_recv()
            b_copy(1, zz, h, False).start()
            s_copy(1 if h == 0 else 2, zz, h, False).start()

    def from_b(zz, step):
        for h in range(2):
            b_copy(0, zz, h, False).wait_recv()
            s_copy(2 if h == 0 else 1, zz, h, False).start()

    def from_ab(zz, step):
        for h in range(2):
            b_copy(1, zz, h, False).wait_recv()
            s_copy(3, zz, h, False).start()

    for turn in range(depth + 2):
        if turn < depth:
            each(turn, along_z)
        if 1 <= turn <= depth:
            each(turn - 1, from_a)
            each(turn - 1, from_b)
        if turn >= 2:
            each(turn - 2, from_ab)

    own_copy.wait()

    def finish(zz, step):
        for h in range(2):
            if step <= 0:

                @pl.when(z < depth - 1)
                def _(h=h):
                    z_copy(zz, h, 1, False).wait_send()

            if step >= 0:

                @pl.when(z > 0)
                def _(h=h):
                    z_copy(zz, h, -1, False).wait_send()

            a_copy(zz, h, False).wait_send()
            for c in range(2):
                b_copy(c, zz, h, False).wait_send()
            for c in range(4):
                s_copy(c, zz, h, False).wait()

    for level in range(depth):
        each(level, finish)


def pack_kernel(rhs2, band_hbm, pos_hbm, normal_hbm, weight_hbm, density_hbm, out_ref, band_ref, pos_ref, normal_ref, weight_ref, density_ref, sems):
    pairs = (
        (band_hbm, band_ref),
        (pos_hbm, pos_ref),
        (normal_hbm, normal_ref),
        (weight_hbm, weight_ref),
        (density_hbm, density_ref),
    )
    copies = [pltpu.make_async_copy(src, dst, sems.at[i]) for i, (src, dst) in enumerate(pairs)]
    for copy in copies:
        copy.start()
    for copy in copies:
        copy.wait()
    _, rounds, band_size = band_ref.shape
    lane = lax.broadcasted_iota(jnp.int32, (1, TILE), 1)
    for t in range(out_ref.shape[1]):
        lanes = pl.ds(t * TILE, TILE)
        out_ref[0, t, :rhs2] = density_ref[:, lanes]
        out_ref[0, t, rhs2 : rhs2 + 3] = pos_ref[:, lanes] * wave_number
        out_ref[0, t, rhs2 + 3 : rhs2 + 6] = normal_ref[:, lanes] * wave_number
        out_ref[0, t, rhs2 + 6 : rhs2 + 7] = weight_ref[:, lanes] * (wave_number / (4.0 * math.pi))
        bands = jnp.zeros((1, TILE), jnp.int32)
        for k in range(t * TILE, min((t + 1) * TILE, rounds * band_size)):
            bands = jnp.where(lane == k - t * TILE, band_ref[0, k // band_size, k % band_size], bands)
        out_ref[0, t, rhs2 + 7 : rhs2 + 8] = bands.astype(jnp.float32)


def gather_blocks(payload, n_dom, n_tgt):
    if n_tgt != 2 or n_dom % 4 or n_dom > 16 or payload.shape[1] % 2:
        return lax.all_gather(payload[0], ("dom", "tgt"), axis=0, tiled=False)
    depth = n_dom // 4
    dma = pltpu.SemaphoreType.DMA
    return pl.pallas_call(
        functools.partial(gather_kernel, n_dom, depth),
        out_shape=jax.ShapeDtypeStruct((n_dom * n_tgt, *payload.shape[1:]), jnp.float32),
        in_specs=[pl.BlockSpec(memory_space=pltpu.VMEM)],
        out_specs=pl.BlockSpec(memory_space=pltpu.VMEM),
        scratch_shapes=[
            dma((2, depth)),
            dma((2, depth)),
            dma((2, 2, depth)),
            dma((2, 4, depth)),
            dma((2, depth)),
            dma((2, depth)),
            dma((2, depth)),
            dma((2, 2, depth)),
            dma((2, 4, depth)),
            dma,
        ],
        compiler_params=pltpu.CompilerParams(collective_id=0, has_side_effects=True, vmem_limit_bytes=8 << 20),
    )(payload)


def entry_kernel(
    n_tgt, rhs2, band_size, near_ref, count_ref, flag_ref, partner_ref, own_ref, all_ref, out_ref, xb, kbuf, left, band_ref, band_sem
):
    local_tiles, max_near = near_ref.shape
    rounds = partner_ref.shape[1]
    part_tiles = local_tiles * n_tgt
    me = lax.axis_index("dom")
    half_rows = rhs2 // 2
    copies = [
        pltpu.make_async_copy(
            all_ref.at[partner_ref[0, r] * n_tgt, c, rhs2 + 7],
            band_ref.at[r, pl.ds(c * TILE, TILE)],
            band_sem.at[r, c],
        )
        for r in range(rounds)
        for c in range(band_ref.shape[1] // TILE)
    ]
    for copy in copies:
        copy.start()
    kbuf[...] = jnp.zeros_like(kbuf)
    for copy in copies:
        copy.wait()

    def one_tile(t, _):
        lanes = pl.ds(pl.multiple_of(t * TILE, TILE), TILE)
        for c in range(3):
            row = own_ref[0, t, pl.ds(rhs2 + c, 1), :]
            xb[c] = jnp.broadcast_to(row, (TILE, TILE)).T
        used = count_ref[t]
        left[...] = jnp.zeros_like(left)

        def locate(j):
            pick = near_ref[t, j]
            beyond = jnp.maximum(pick - part_tiles, 0)
            other = partner_ref[0, beyond // band_size]
            far_tile = band_ref[beyond // band_size, beyond].astype(jnp.int32)
            is_own = pick < part_tiles
            tile = jnp.where(is_own, pick, far_tile)
            dom = jnp.where(is_own, me, other)
            return dom * n_tgt + tile // local_tiles, tile % local_tiles

        def add_pair(i, total):
            total = total + lax.dot_general(
                left[...], kbuf[...], (((1,), (1,)), ((), ())), preferred_element_type=jnp.float32
            )
            for e in range(2):
                j = 2 * i + e
                jj = jnp.minimum(j, max_near - 1)
                block, tile = locate(jj)
                core = jnp.where(flag_ref[t, jj] > 0, wide_core, narrow_core) * wave_number
                core_sq = core * core
                valid = jnp.where(j < used, 1.0, 0.0)
                real = all_ref[block, tile, pl.ds(0, half_rows), :]
                imag = all_ref[block, tile, pl.ds(half_rows, half_rows), :]
                base = 2 * TILE * e
                left[:half_rows, base : base + TILE] = (-real).astype(jnp.bfloat16)
                left[:half_rows, base + TILE : base + 2 * TILE] = (-imag).astype(jnp.bfloat16)
                left[half_rows:, base : base + TILE] = (-imag).astype(jnp.bfloat16)
                left[half_rows:, base + TILE : base + 2 * TILE] = real.astype(jnp.bfloat16)
                rows = [
                    jnp.broadcast_to(all_ref[block, tile, pl.ds(rhs2 + c, 1), :], (CHUNK, TILE)) for c in range(7)
                ]
                weight = rows[6] * valid
                for k in range(TILE // CHUNK):
                    part = pl.ds(k * CHUNK, CHUNK)
                    dx = rows[0] - xb[0, part]
                    dy = rows[1] - xb[1, part]
                    dz = rows[2] - xb[2, part]
                    d_sq = (dx * dx + core_sq) + (dy * dy + dz * dz)
                    along = dx * rows[3] + dy * rows[4] + dz * rows[5]
                    inverse = lax.rsqrt(d_sq)
                    turns = d_sq * (inverse * (0.5 / math.pi))
                    frac = turns - jnp.round(turns)
                    z = frac * frac
                    s = frac * poly(SIN_POLY, z)
                    sin = s * poly(COS_POLY, z)
                    cos = 1.0 - s * s
                    slope = along * inverse
                    radial = inverse * weight
                    a = slope * inverse * radial
                    b = (slope + coupling) * radial
                    kbuf[part, base : base + TILE] = (cos * a + sin * b).astype(jnp.bfloat16)
                    kbuf[part, base + TILE : base + 2 * TILE] = (cos * b - sin * a).astype(jnp.bfloat16)
            return total

        total = lax.fori_loop(0, (used + 1) // 2, add_pair, jnp.zeros((rhs2, TILE), jnp.float32))
        total = total + lax.dot_general(
            left[...], kbuf[...], (((1,), (1,)), ((), ())), preferred_element_type=jnp.float32
        )
        out_ref[:, lanes] = total
        return 0

    lax.fori_loop(0, local_tiles, one_tile, 0)


def shards(
    positions, normals, weights, density, partners, band_list, near_list, near_count, singular
):
    n_dom, n_tgt = lax.axis_size("dom"), lax.axis_size("tgt")
    points = positions.shape[1]
    rhs2 = density.shape[0]
    rounds, band_size = band_list.shape[1:]
    bands = rounds * band_size
    smem = pl.BlockSpec(memory_space=pltpu.SMEM)
    vmem = pl.BlockSpec(memory_space=pltpu.VMEM)
    payload = pl.pallas_call(
        functools.partial(pack_kernel, rhs2),
        out_shape=jax.ShapeDtypeStruct((1, points // TILE, rhs2 + 8, TILE), jnp.float32),
        in_specs=[pl.BlockSpec(memory_space=pltpu.HBM)] * 5,
        out_specs=vmem,
        scratch_shapes=[
            pltpu.SMEM(band_list.shape, jnp.int32),
            pltpu.VMEM(positions.shape, jnp.float32),
            pltpu.VMEM(normals.shape, jnp.float32),
            pltpu.VMEM((1, points), jnp.float32),
            pltpu.VMEM(density.shape, jnp.float32),
            pltpu.SemaphoreType.DMA((5,)),
        ],
        compiler_params=pltpu.CompilerParams(vmem_limit_bytes=4 << 20),
    )(*[pltpu.with_memory_space_constraint(a, pltpu.HBM) for a in (band_list, positions, normals, weights[None, :], density)])
    blocks = gather_blocks(payload, n_dom, n_tgt)
    band_lanes = -(-bands // TILE) * TILE
    return pl.pallas_call(
        functools.partial(entry_kernel, n_tgt, rhs2, band_size),
        out_shape=jax.ShapeDtypeStruct((rhs2, points), jnp.float32),
        in_specs=[smem] * 4 + [vmem] * 2,
        out_specs=vmem,
        scratch_shapes=[
            pltpu.VMEM((3, TILE, TILE), jnp.float32),
            pltpu.VMEM((TILE, 4 * TILE), jnp.bfloat16),
            pltpu.VMEM((rhs2, 4 * TILE), jnp.bfloat16),
            pltpu.SMEM((rounds, band_lanes), jnp.float32),
            pltpu.SemaphoreType.DMA((rounds, band_lanes // TILE)),
        ],
        compiler_params=pltpu.CompilerParams(vmem_limit_bytes=4 * blocks.size + (6 << 20)),
    )(near_list, near_count, singular, partners, payload, blocks)


def solution(mesh):
    in_specs = (
        P(None, ("dom", "tgt")),
        P(None, ("dom", "tgt")),
        P(("dom", "tgt")),
        P(None, ("dom", "tgt")),
        P("dom", None),
        P("dom", None, None),
        P(("dom", "tgt"), None),
        P(("dom", "tgt")),
        P(("dom", "tgt"), None),
    )
    out_specs = P(None, ("dom", "tgt"))
    return jax.shard_map(shards, mesh=mesh, in_specs=in_specs, out_specs=out_specs, check_vma=False)
```
